32 devices in a mesh: dp: 4 (over y, x), fsdp: 8 (over z, core).
Axes of the slice: x: 2, y: 2, z: 4, core: 2. Of those that a mesh axis runs over, the one named last changes fastest.
Arguments:
- tokens: bfloat16 [8, 512, 2048], P('fsdp', 'dp'), may hold values from -6 to 6
- attn_gain: bfloat16 [2048], P(('dp', 'fsdp')), may hold values from 0.5 to 1.5
- query_weight: bfloat16 [2048, 2048], P(('dp', 'fsdp')), may hold values from -0.125 to 0.125
- kv_weight: bfloat16 [2048, 256], P(('dp', 'fsdp')), may hold values from -0.125 to 0.125
- out_weight: bfloat16 [2048, 2048], P(('dp', 'fsdp')), may hold values from -1 to 1
- mlp_gain: bfloat16 [2048], P(('dp', 'fsdp')), may hold values from 0.5 to 1.5
- gate_weight: bfloat16 [2048, 5632], P(('dp', 'fsdp')), may hold values from -0.125 to 0.125
- up_weight: bfloat16 [2048, 5632], P(('dp', 'fsdp')), may hold values from -0.125 to 0.125
- down_weight: bfloat16 [2048, 5632], P(('dp', 'fsdp')), may hold values from -0.078125 to 0.078125
- seq_group: int32 [8], P('fsdp'), may hold values from 0 to 7
- group_weight: float32 [8], replicated, may hold values from 0.5 to 2
- out_grad: bfloat16 [8, 512, 2048], P('fsdp', 'dp'), may hold values from -6 to 6
- kv_grad: bfloat16 [8, 512, 256], P('fsdp', 'dp'), may hold values from -6 to 6
Outputs:
- layer_out: bfloat16 [8, 512, 2048], P('fsdp', 'dp')
- shared_kv: bfloat16 [8, 512, 256], P('fsdp', 'dp')
- input_grad: float32 [8, 512, 2048], P('fsdp', 'dp')
- attn_gain_grad: float32 [2048], P(('dp', 'fsdp'))
- query_weight_grad: float32 [2048, 2048], P(('dp', 'fsdp'))
- kv_weight_grad: float32 [2048, 256], P(('dp', 'fsdp'))
- out_weight_grad: float32 [2048, 2048], P(('dp', 'fsdp'))
- mlp_gain_grad: float32 [2048], P(('dp', 'fsdp'))
- gate_weight_grad: float32 [2048, 5632], P(('dp', 'fsdp'))
- up_weight_grad: float32 [2048, 5632], P(('dp', 'fsdp'))
- down_weight_grad: float32 [2048, 5632], P(('dp', 'fsdp'))
The draws below stay inside these ranges and needn't reach their ends.
All inputs are finite; a program needn't handle non-finite values.
Results may differ from the reference program's by a relative error of at most 0.015.
Values may be sent and summed in bfloat16 or wider, within the bound.
No kernel may reach another device: no remote copies, remote signals or barrier semaphores. Data moves between devices by JAX's collectives and lax.ppermute only.
A program may use at most 512 MiB of HBM per device.

```python
import math
import jax
import jax.numpy as jnp
from jax import lax

D = 2048
HEADS = 16
HD = 128
FF = 5632
GROUPS = 8
HQ = 2048
KV = 256
SEQS = 8
LEN = 512
TOKENS = 4096


def plant(entries, stream_key, low, top_value):
    longest = entries.shape.index(max(entries.shape))
    spots = []
    for shift in (0, 1):
        where = [jax.random.randint(jax.random.fold_in(stream_key, axis), (), 0, length) for axis, length in enumerate(entries.shape)]
        where[longest] = (where[longest] + shift) % entries.shape[longest]
        spots.append(tuple(where))
    return entries.at[spots[0]].set(low).at[spots[1]].set(top_value)


def strengthened(entries, key, source, target, blocks, factor):
    def block_of(axis_at):
        return (jnp.arange(entries.shape[axis_at]) // (entries.shape[axis_at] // blocks)).reshape((-1,) + (1,) * (entries.ndim - 1 - axis_at))

    first = jax.random.permutation(key, blocks)[block_of(target)]
    second = (block_of(target) + blocks // 2) % blocks
    return jnp.where((block_of(source) == first) | (block_of(source) == second), factor * entries, entries)


def block_scale(own_key, shape, split, smallest, largest):
    def one(axis_at, shards_of):
        steps = jax.random.uniform(jax.random.fold_in(jax.random.fold_in(own_key, 6), axis_at), (shards_of,), jnp.float32, smallest / len(split), largest / len(split))
        return jnp.repeat(jnp.exp(steps), shape[axis_at] // shards_of).reshape((-1,) + (1,) * (len(shape) - axis_at - 1))

    loudness = one(*split[0])
    for cut in split[1:]:
        loudness = loudness * one(*cut)
    return loudness


def normal_values(rng, extent, deviation, reach, pieces=(), held_as=jnp.bfloat16):
    result = deviation * jax.random.normal(rng, extent, jnp.float32)
    if pieces:
        result = result * block_scale(rng, extent, pieces, -0.22, 0.18)
    return jnp.clip(result, -reach, reach).astype(held_as)


def heavy_noise(stream_key, shape, spread, most, shards, heavy, kind=jnp.bfloat16):
    array = spread * jax.random.normal(stream_key, shape, jnp.float32)
    if shards:
        array = array * block_scale(stream_key, shape, shards, -0.22, 0.18)
    return jnp.clip(strengthened(array, jax.random.fold_in(stream_key, 3), *heavy), -most, most).astype(kind)


def setup_inputs(seed: int = 0) -> dict:
    keys = jax.random.split(jax.random.key(seed), 14)
    tokens = normal_values(keys[0], (SEQS, LEN, D), 1.0, 6.0, ((0, 8), (1, 4)))
    attn_gain = jnp.clip(1.0 + 0.1 * jax.random.normal(keys[1], (D,), jnp.float32), 0.5, 1.5).astype(jnp.bfloat16)
    query_weight = normal_values(keys[2], (D, HQ), D ** -0.5, 0.125, ((0, 32),))
    kv_weight = normal_values(keys[3], (D, KV), D ** -0.5, 0.125, ((0, 32),))
    out_weight = normal_values(keys[4], (D, HQ), (max(HQ // 64, 4)) ** -0.5, 1.0, ((0, 32),))
    mlp_gain = jnp.clip(1.0 + 0.1 * jax.random.normal(keys[5], (D,), jnp.float32), 0.5, 1.5).astype(jnp.bfloat16)
    gate_weight = normal_values(keys[6], (D, FF), D ** -0.5, 0.125, ((0, 32),))
    up_weight = normal_values(keys[7], (D, FF), D ** -0.5, 0.125, ((0, 32),))
    down_weight = normal_values(keys[8], (D, FF), FF ** -0.5, 0.078125, ((0, 32),))
    seq_group = plant(jax.random.randint(keys[9], (SEQS,), 0, GROUPS), jax.random.fold_in(keys[9], 1), 0, GROUPS - 1).astype(jnp.int32)
    group_weight = jnp.clip(jnp.exp(jax.random.uniform(keys[10], (GROUPS,), jnp.float32, math.log(0.5), math.log(2.0))), 0.5, 2.0)
    out_grad = heavy_noise(keys[11], (SEQS, LEN, D), 1.0, 6.0, ((0, 8), (1, 4)), (0, 2, 8, 2.0))
    kv_grad = normal_values(keys[12], (SEQS, LEN, KV), 1.0, 6.0, ((0, 8), (1, 4)))
    return dict(tokens=tokens, attn_gain=attn_gain, query_weight=query_weight, kv_weight=kv_weight, out_weight=out_weight, mlp_gain=mlp_gain, gate_weight=gate_weight, up_weight=up_weight, down_weight=down_weight, seq_group=seq_group, group_weight=group_weight, out_grad=out_grad, kv_grad=kv_grad)


norm_eps = 1e-05
rope_base = 10000.0
masked_score = -1e+30
highest = lax.Precision.HIGHEST

@jax.custom_vjp
def low(v):
    return lax.optimization_barrier(v.astype(jnp.bfloat16)).astype(jnp.float32)

@jax.custom_vjp
def low_back(v):
    return v

def low_keep(v):
    return (low(v), None)

def low_pass(kept, grad):
    return (grad,)

def back_keep(v):
    return (v, None)

def back_low(kept, grad):
    return (low(grad),)
low.defvjp(low_keep, low_pass)
low_back.defvjp(back_keep, back_low)

def rope_tables(positions, half_width):
    index_vec = jnp.arange(half_width, dtype=jnp.float32)
    frequency = jnp.power(rope_base, -(2.0 * index_vec) / (2 * half_width))
    angles = positions.astype(jnp.float32)[:, None] * frequency[None, :]
    return (jnp.cos(angles), jnp.sin(angles))

def rotate(values, cos_vals, sin_vals):
    half_width = values.shape[-1] // 2
    first_half = values[..., :half_width]
    second_half = values[..., half_width:]
    return jnp.concatenate([first_half * cos_vals - second_half * sin_vals, second_half * cos_vals + first_half * sin_vals], axis=-1)

def rms_scale(values):
    return values * lax.rsqrt(lax.optimization_barrier(jnp.mean(values * values, axis=-1, keepdims=True)) + norm_eps)

def matmul(left_rows, right_cols):
    return jnp.dot(left_rows, right_cols, precision=highest, preferred_element_type=jnp.float32)

def attend(seq_pair):
    queries, shared = seq_pair
    scores = low_back(jnp.einsum('thd,kd->thk', queries, shared[:, :HD], precision=highest))
    places = jnp.arange(queries.shape[0], dtype=jnp.int32)
    visible = places[None, :] <= places[:, None]
    scores = jnp.where(visible[:, None, :], scores, masked_score)
    prob_vals = low(jax.nn.softmax(scores, axis=-1))
    return jnp.einsum('thk,kd->thd', prob_vals, shared[:, HD:], precision=highest)

def forward(tokens, attn_gain, query_weight, kv_weight, out_weight, mlp_gain, gate_weight, up_weight, down_weight):
    flat_in = tokens.reshape(TOKENS, D)
    normed_one = low(rms_scale(flat_in) * attn_gain)
    query_pre = low_back(matmul(normed_one, query_weight))
    kv_pre = low_back(matmul(normed_one, kv_weight))
    cos_vals, sin_vals = rope_tables(jnp.arange(LEN, dtype=jnp.int32), HD // 2)
    queries = query_pre.reshape(SEQS, LEN, HEADS, HD)
    queries = low(rotate(queries, cos_vals[None, :, None, :], sin_vals[None, :, None, :]) * HD ** (-0.5))
    kv_seq = kv_pre.reshape(SEQS, LEN, KV)
    key_rot = rotate(kv_seq[..., :HD], cos_vals[None], sin_vals[None])
    shared = low(jnp.concatenate([key_rot, kv_seq[..., HD:]], axis=-1))
    attended = lax.map(jax.checkpoint(attend), (queries, shared))
    attn_rows = low(low_back(attended)).reshape(TOKENS, HQ)
    attn_branch = low_back(matmul(attn_rows, out_weight.T))
    middle = flat_in + attn_branch
    normed_two = low(rms_scale(middle) * mlp_gain)
    gate_pre = low_back(matmul(normed_two, gate_weight))
    up_pre = low_back(matmul(normed_two, up_weight))
    hidden = low(jax.nn.silu(gate_pre) * up_pre)
    mlp_branch = low_back(matmul(hidden, down_weight.T))
    return ((middle + mlp_branch).reshape(SEQS, LEN, D), shared)

def reference(tokens, attn_gain, query_weight, kv_weight, out_weight, mlp_gain, gate_weight, up_weight, down_weight, seq_group, group_weight, out_grad, kv_grad):
    primals = tuple((source.astype(jnp.float32) for source in (tokens, attn_gain, query_weight, kv_weight, out_weight, mlp_gain, gate_weight, up_weight, down_weight)))
    (block_out, shared), pullback = jax.vjp(forward, *primals)
    chosen = seq_group[:, None] == jnp.arange(GROUPS, dtype=jnp.int32)[None, :]
    seq_weight = lax.optimization_barrier(jnp.sum(jnp.where(chosen, group_weight[None, :], 0.0), axis=1))
    gradients = pullback((out_grad.astype(jnp.float32) * seq_weight[:, None, None], kv_grad.astype(jnp.float32)))
    return (block_out.astype(jnp.bfloat16), shared.astype(jnp.bfloat16), gradients[0], gradients[1], gradients[2], gradients[3], gradients[4], gradients[5], gradients[6], gradients[7], gradients[8])
```

```python
import jax
import jax.numpy as jnp
from jax import lax
from jax.sharding import PartitionSpec as P

norm_eps = 1e-05
rope_base = 10000.0
masked_score = -1e30
f32 = jnp.float32
bf16 = jnp.bfloat16


def rope_tables(positions, half_width):
    index_vec = jnp.arange(half_width, dtype=f32)
    frequency = jnp.power(rope_base, -(2.0 * index_vec) / (2 * half_width))
    angles = positions.astype(f32)[:, None] * frequency[None, :]
    return (jnp.cos(angles), jnp.sin(angles))


def rotate(values, cos_vals, sin_vals):
    half_width = values.shape[-1] // 2
    first_half = values[..., :half_width]
    second_half = values[..., half_width:]
    return jnp.concatenate(
        [
            first_half * cos_vals - second_half * sin_vals,
            second_half * cos_vals + first_half * sin_vals,
        ],
        axis=-1,
    )


def rotate_back(values, cos_vals, sin_vals):
    return rotate(values, cos_vals, -sin_vals)


def norm_back(grad_hat, normed_hat, inv_rms):
    inner_mean = jnp.mean(grad_hat * normed_hat, axis=1, keepdims=True)
    return inv_rms * (grad_hat - normed_hat * inner_mean)


def mm(left, right):
    return jnp.dot(left, right, preferred_element_type=f32)


def mm_nt(left, right):
    return lax.dot_general(left, right, (((1,), (1,)), ((), ())), preferred_element_type=f32)


def mm_tn(left, right):
    return lax.dot_general(left, right, (((0,), (0,)), ((), ())), preferred_element_type=f32)


def local(
    tokens,
    attn_gain,
    query_weight,
    kv_weight,
    out_weight,
    mlp_gain,
    gate_weight,
    up_weight,
    down_weight,
    seq_group,
    group_weight,
    out_grad,
    kv_grad,
):
    dp_size = lax.axis_size("dp")
    fsdp_size = lax.axis_size("fsdp")
    dp_index = lax.axis_index("dp")
    tok_rows, model_width = tokens.shape[1:]
    own_rows = query_weight.shape[0]
    head_width = kv_weight.shape[1] // 2
    kv_width = 2 * head_width
    query_cols = query_weight.shape[1] // dp_size
    head_count = query_cols // head_width
    ff_cols = gate_weight.shape[1] // dp_size
    score_scale = head_width ** (-0.5)

    def permuted(rows):
        blocks = rows.reshape(rows.shape[0], dp_size, fsdp_size, own_rows)
        return blocks.transpose(0, 2, 1, 3).reshape(rows.shape)

    def unpermuted(rows):
        blocks = rows.reshape(rows.shape[0], fsdp_size, dp_size, own_rows)
        return blocks.transpose(0, 2, 1, 3).reshape(rows.shape)

    def peers(step):
        return [(i, i ^ step) for i in range(dp_size)]

    def gathered(block):
        blocks = [block] + [lax.ppermute(block, "dp", peers(k)) for k in range(1, dp_size)]
        return jnp.concatenate(blocks, axis=0)

    def scattered(partial):
        rows = partial.shape[0] // dp_size
        total = partial[:rows]
        for k in range(1, dp_size):
            part = partial[k * rows : (k + 1) * rows].astype(bf16)
            total = total + lax.ppermute(part, "dp", peers(k)).astype(f32)
        return total

    def column_blocks(matrix):
        cols = matrix.shape[1] // dp_size
        return matrix.reshape(own_rows, dp_size, cols).transpose(1, 0, 2)

    def exchanged(packed):
        return lax.all_to_all(packed, "dp", 0, 0)

    def all_rows(packed):
        return lax.all_gather(
            packed.reshape(dp_size * own_rows, packed.shape[2]), "fsdp", axis=0, tiled=True
        )

    def own_share(grads):
        share = lax.psum_scatter(grads.astype(bf16), "fsdp", scatter_dimension=0, tiled=True)
        return exchanged(share.reshape(dp_size, own_rows, grads.shape[1])).astype(f32)

    def joined(blocks):
        return blocks.transpose(1, 0, 2).reshape(own_rows, dp_size * blocks.shape[2])

    gain_one = attn_gain.astype(f32)[:, None]
    gain_two = mlp_gain.astype(f32)[:, None]

    def scaled(matrix, gain):
        return (matrix.astype(f32) * gain).astype(bf16)

    attn_pack = jnp.concatenate(
        [
            column_blocks(scaled(query_weight, gain_one)),
            jnp.broadcast_to(scaled(kv_weight, gain_one)[None], (dp_size, own_rows, kv_width)),
            column_blocks(out_weight),
        ],
        axis=2,
    )
    ff_pack = jnp.concatenate(
        [
            column_blocks(scaled(gate_weight, gain_two)),
            column_blocks(scaled(up_weight, gain_two)),
        ],
        axis=2,
    )
    attn_all = all_rows(exchanged(attn_pack))
    ff_all = all_rows(exchanged(ff_pack))
    down_all = all_rows(exchanged(column_blocks(down_weight)))
    query_all = attn_all[:, :query_cols]
    kv_all = attn_all[:, query_cols : query_cols + kv_width]
    out_all = attn_all[:, query_cols + kv_width :]

    def block_positions(k):
        return (dp_index ^ k) * tok_rows + jnp.arange(tok_rows, dtype=jnp.int32)

    positions = jnp.concatenate([block_positions(k) for k in range(dp_size)])
    cos_all, sin_all = rope_tables(positions, head_width // 2)
    cos_own, sin_own = cos_all[:tok_rows], sin_all[:tok_rows]
    seq_len = positions.shape[0]

    inputs = permuted(tokens[0]).astype(f32)
    inv_one = lax.rsqrt(jnp.mean(inputs * inputs, axis=1, keepdims=True) + norm_eps)
    hat_one = inputs * inv_one
    hat_one_low = hat_one.astype(bf16)
    hat_one_seq = gathered(hat_one_low)
    kv_pre = mm(hat_one_low, kv_all)
    key_rot = rotate(kv_pre[:, :head_width], cos_own, sin_own)
    shared = jnp.concatenate([key_rot, kv_pre[:, head_width:]], axis=1).astype(bf16)
    shared_seq = gathered(shared)
    keys, values = shared_seq[:, :head_width], shared_seq[:, head_width:]
    query_pre = mm(hat_one_seq, query_all).reshape(seq_len, head_count, head_width)
    query_rot = rotate(query_pre, cos_all[:, None, :], sin_all[:, None, :])
    queries = (query_rot * score_scale).astype(bf16)
    scores = jnp.einsum("thd,kd->htk", queries, keys, preferred_element_type=f32)
    visible = positions[None, :] <= positions[:, None]
    scores = jnp.where(visible[None], scores, masked_score)
    probs = jax.nn.softmax(scores, axis=-1)
    probs_low = probs.astype(bf16)
    attended = jnp.einsum("htk,kd->thd", probs_low, values, preferred_element_type=f32)
    attn_rows = attended.reshape(seq_len, query_cols).astype(bf16)
    middle = inputs + scattered(mm_nt(attn_rows, out_all))

    inv_two = lax.rsqrt(jnp.mean(middle * middle, axis=1, keepdims=True) + norm_eps)
    hat_two = middle * inv_two
    hat_two_seq = gathered(hat_two.astype(bf16))
    pre = mm(hat_two_seq, ff_all)
    gate_pre, up_pre = pre[:, :ff_cols], pre[:, ff_cols:]
    sigmoid_gate = jax.nn.sigmoid(gate_pre)
    silu_gate = gate_pre * sigmoid_gate
    hidden = (silu_gate * up_pre).astype(bf16)
    layer_out = unpermuted((middle + scattered(mm_nt(hidden, down_all))).astype(bf16))

    group_ids = jnp.arange(group_weight.shape[0], dtype=jnp.int32)
    seq_weight = jnp.sum(jnp.where(group_ids == seq_group[0], group_weight, 0.0))
    grad_out = permuted(out_grad[0]).astype(f32) * seq_weight
    grad_out_seq = gathered(grad_out.astype(bf16))
    grad_hidden = mm(grad_out_seq, down_all)
    grad_gate = grad_hidden * up_pre * sigmoid_gate * (1.0 + gate_pre * (1.0 - sigmoid_gate))
    grad_up = grad_hidden * silu_gate
    grad_ff = jnp.concatenate([grad_gate.astype(bf16), grad_up.astype(bf16)], axis=1)
    down_share = own_share(mm_tn(grad_out_seq, hidden))
    ff_share = own_share(mm_tn(hat_two_seq, grad_ff))
    grad_hat_two = scattered(mm_nt(grad_ff, ff_all))
    grad_middle = grad_out + norm_back(grad_hat_two, hat_two, inv_two)

    grad_mid_seq = gathered(grad_middle.astype(bf16))
    grad_heads = mm(grad_mid_seq, out_all).astype(bf16).reshape(seq_len, head_count, head_width)
    row_dot = jnp.sum(grad_heads.astype(f32) * attended, axis=2)
    grad_probs = jnp.einsum("thd,kd->htk", grad_heads, values, preferred_element_type=f32)
    grad_scores = (probs * (grad_probs - row_dot.T[:, :, None])).astype(bf16)
    grad_query = jnp.einsum("htk,kd->thd", grad_scores, keys, preferred_element_type=f32)
    grad_keys = jnp.einsum("htk,thd->kd", grad_scores, queries, preferred_element_type=f32)
    grad_values = jnp.einsum("htk,thd->kd", probs_low, grad_heads, preferred_element_type=f32)
    kv_total = scattered(jnp.concatenate([grad_keys, grad_values], axis=1))
    kv_total = kv_total + kv_grad[0].astype(f32)
    key_back = rotate_back(kv_total[:, :head_width], cos_own, sin_own)
    grad_kv_pre = jnp.concatenate([key_back, kv_total[:, head_width:]], axis=1).astype(bf16)
    query_back = rotate_back(grad_query * score_scale, cos_all[:, None, :], sin_all[:, None, :])
    grad_query_pre = query_back.reshape(seq_len, query_cols).astype(bf16)
    grad_hat_one = scattered(mm_nt(grad_query_pre, query_all)) + mm_nt(grad_kv_pre, kv_all)
    input_grad = unpermuted(grad_middle + norm_back(grad_hat_one, hat_one, inv_one))
    attn_share = own_share(
        jnp.concatenate(
            [
                mm_tn(hat_one_seq, grad_query_pre).astype(bf16),
                mm_tn(hat_one_low, grad_kv_pre).astype(bf16),
                mm_tn(grad_mid_seq, attn_rows).astype(bf16),
            ],
            axis=1,
        )
    )
    query_raw = joined(attn_share[:, :, :query_cols])
    kv_raw = jnp.sum(attn_share[:, :, query_cols : query_cols + kv_width], axis=0)
    out_weight_grad = joined(attn_share[:, :, query_cols + kv_width :])
    gate_raw = joined(ff_share[:, :, :ff_cols])
    up_raw = joined(ff_share[:, :, ff_cols:])

    def row_sum(raw, matrix):
        return jnp.sum(raw * matrix.astype(f32), axis=1)

    return (
        layer_out[None],
        shared[None],
        input_grad[None],
        row_sum(query_raw, query_weight) + row_sum(kv_raw, kv_weight),
        query_raw * gain_one,
        kv_raw * gain_one,
        out_weight_grad,
        row_sum(gate_raw, gate_weight) + row_sum(up_raw, up_weight),
        gate_raw * gain_two,
        up_raw * gain_two,
        joined(down_share),
    )


def solution(mesh):
    rows = P("fsdp", "dp", None)
    gain = P(("dp", "fsdp"))
    matrix = P(("dp", "fsdp"), None)
    return jax.shard_map(
        local,
        mesh=mesh,
        in_specs=(
            rows,
            gain,
            matrix,
            matrix,
            matrix,
            gain,
            matrix,
            matrix,
            matrix,
            P("fsdp"),
            P(),
            rows,
            rows,
        ),
        out_specs=(
            rows,
            rows,
            rows,
            gain,
            matrix,
            matrix,
            matrix,
            gain,
            matrix,
            matrix,
            matrix,
        ),
        check_vma=False,
    )
```

```python
import jax
import jax.numpy as jnp
from jax import lax
from jax.sharding import PartitionSpec as P

norm_eps = 1e-05
rope_base = 10000.0
masked_score = -1e30
f32 = jnp.float32
bf16 = jnp.bfloat16


def rope_tables(positions, half_width):
    index_vec = jnp.arange(half_width, dtype=f32)
    frequency = jnp.power(rope_base, -(2.0 * index_vec) / (2 * half_width))
    angles = positions.astype(f32)[:, None] * frequency[None, :]
    return (jnp.cos(angles), jnp.sin(angles))


def rotate(values, cos_vals, sin_vals):
    half_width = values.shape[-1] // 2
    first_half = values[..., :half_width]
    second_half = values[..., half_width:]
    return jnp.concatenate(
        [
            first_half * cos_vals - second_half * sin_vals,
            second_half * cos_vals + first_half * sin_vals,
        ],
        axis=-1,
    )


def rotate_back(values, cos_vals, sin_vals):
    return rotate(values, cos_vals, -sin_vals)


def norm_back(grad_hat, normed_hat, inv_rms):
    inner_mean = jnp.mean(grad_hat * normed_hat, axis=1, keepdims=True)
    return inv_rms * (grad_hat - normed_hat * inner_mean)


def mm(left, right):
    return jnp.dot(left, right, preferred_element_type=f32)


def mm_nt(left, right):
    return lax.dot_general(left, right, (((1,), (1,)), ((), ())), preferred_element_type=f32)


def mm_tn(left, right):
    return lax.dot_general(left, right, (((0,), (0,)), ((), ())), preferred_element_type=f32)


def local(
    tokens,
    attn_gain,
    query_weight,
    kv_weight,
    out_weight,
    mlp_gain,
    gate_weight,
    up_weight,
    down_weight,
    seq_group,
    group_weight,
    out_grad,
    kv_grad,
):
    dp_size = lax.axis_size("dp")
    fsdp_size = lax.axis_size("fsdp")
    dp_index = lax.axis_index("dp")
    tok_rows, model_width = tokens.shape[1:]
    own_rows = query_weight.shape[0]
    head_width = kv_weight.shape[1] // 2
    kv_width = 2 * head_width
    query_cols = query_weight.shape[1] // dp_size
    head_count = query_cols // head_width
    ff_cols = gate_weight.shape[1] // dp_size
    score_scale = head_width ** (-0.5)

    def permuted(rows):
        blocks = rows.reshape(rows.shape[0], dp_size, fsdp_size, own_rows)
        return blocks.transpose(0, 2, 1, 3).reshape(rows.shape)

    def unpermuted(rows):
        blocks = rows.reshape(rows.shape[0], fsdp_size, dp_size, own_rows)
        return blocks.transpose(0, 2, 1, 3).reshape(rows.shape)

    def peers(step):
        return [(i, i ^ step) for i in range(dp_size)]

    def gathered(block):
        blocks = [block] + [lax.ppermute(block, "dp", peers(k)) for k in range(1, dp_size)]
        return jnp.concatenate(blocks, axis=0)

    def scattered(partial):
        rows = partial.shape[0] // dp_size
        total = partial[:rows]
        for k in range(1, dp_size):
            part = partial[k * rows : (k + 1) * rows].astype(bf16)
            total = total + lax.ppermute(part, "dp", peers(k)).astype(f32)
        return total

    def column_blocks(matrix):
        cols = matrix.shape[1] // dp_size
        return matrix.reshape(own_rows, dp_size, cols).transpose(1, 0, 2)

    def exchanged(packed):
        return lax.all_to_all(packed, "dp", 0, 0)

    def all_rows(packed):
        return lax.all_gather(
            packed.reshape(dp_size * own_rows, packed.shape[2]), "fsdp", axis=0, tiled=True
        )

    def summed(grads):
        return lax.psum_scatter(grads.astype(bf16), "fsdp", scatter_dimension=0, tiled=True)

    def own_share(share):
        return exchanged(share.reshape(dp_size, own_rows, share.shape[1])).astype(f32)

    def joined(blocks):
        return blocks.transpose(1, 0, 2).reshape(own_rows, dp_size * blocks.shape[2])

    gain_one = attn_gain.astype(f32)[:, None]
    gain_two = mlp_gain.astype(f32)[:, None]

    def scaled(matrix, gain):
        return (matrix.astype(f32) * gain).astype(bf16)

    attn_pack = jnp.concatenate(
        [
            column_blocks(scaled(query_weight, gain_one)),
            jnp.broadcast_to(scaled(kv_weight, gain_one)[None], (dp_size, own_rows, kv_width)),
            column_blocks(out_weight),
        ],
        axis=2,
    )
    ff_pack = jnp.concatenate(
        [
            column_blocks(scaled(gate_weight, gain_two)),
            column_blocks(scaled(up_weight, gain_two)),
        ],
        axis=2,
    )
    attn_all = all_rows(exchanged(attn_pack))
    ff_all = all_rows(exchanged(ff_pack))
    down_all = all_rows(exchanged(column_blocks(down_weight)))
    query_all = attn_all[:, :query_cols]
    kv_all = attn_all[:, query_cols : query_cols + kv_width]
    out_all = attn_all[:, query_cols + kv_width :]

    def block_positions(k):
        return (dp_index ^ k) * tok_rows + jnp.arange(tok_rows, dtype=jnp.int32)

    positions = jnp.concatenate([block_positions(k) for k in range(dp_size)])
    cos_all, sin_all = rope_tables(positions, head_width // 2)
    cos_own, sin_own = cos_all[:tok_rows], sin_all[:tok_rows]
    seq_len = positions.shape[0]

    inputs = permuted(tokens[0]).astype(f32)
    inv_one = lax.rsqrt(jnp.mean(inputs * inputs, axis=1, keepdims=True) + norm_eps)
    hat_one = inputs * inv_one
    hat_one_low = hat_one.astype(bf16)
    hat_one_seq = gathered(hat_one_low)
    kv_pre = mm(hat_one_low, kv_all)
    key_rot = rotate(kv_pre[:, :head_width], cos_own, sin_own)
    shared = jnp.concatenate([key_rot, kv_pre[:, head_width:]], axis=1).astype(bf16)
    shared_seq = gathered(shared)
    keys, values = shared_seq[:, :head_width], shared_seq[:, head_width:]
    query_pre = mm(hat_one_seq, query_all).reshape(seq_len, head_count, head_width)
    query_rot = rotate(query_pre, cos_all[:, None, :], sin_all[:, None, :])
    queries = (query_rot * score_scale).astype(bf16)
    scores = jnp.einsum("thd,kd->htk", queries, keys, preferred_element_type=f32)
    visible = positions[None, :] <= positions[:, None]
    scores = jnp.where(visible[None], scores, masked_score)
    probs = jax.nn.softmax(scores, axis=-1)
    probs_low = probs.astype(bf16)
    attended = jnp.einsum("htk,kd->thd", probs_low, values, preferred_element_type=f32)
    attn_rows = attended.reshape(seq_len, query_cols).astype(bf16)
    middle = inputs + scattered(mm_nt(attn_rows, out_all))

    inv_two = lax.rsqrt(jnp.mean(middle * middle, axis=1, keepdims=True) + norm_eps)
    hat_two = middle * inv_two
    hat_two_seq = gathered(hat_two.astype(bf16))
    pre = mm(hat_two_seq, ff_all)
    gate_pre, up_pre = pre[:, :ff_cols], pre[:, ff_cols:]
    sigmoid_gate = jax.nn.sigmoid(gate_pre)
    silu_gate = gate_pre * sigmoid_gate
    hidden = (silu_gate * up_pre).astype(bf16)

    group_ids = jnp.arange(group_weight.shape[0], dtype=jnp.int32)
    seq_weight = jnp.sum(jnp.where(group_ids == seq_group[0], group_weight, 0.0))
    grad_out = permuted(out_grad[0]).astype(f32) * seq_weight
    grad_out_seq = gathered(grad_out.astype(bf16))
    down_grad = mm_tn(grad_out_seq, hidden).astype(bf16)
    down_all, down_grad = lax.optimization_barrier((down_all, down_grad))
    down_sum = summed(down_grad)
    grad_hidden = mm(grad_out_seq, down_all)
    grad_gate = grad_hidden * up_pre * sigmoid_gate * (1.0 + gate_pre * (1.0 - sigmoid_gate))
    grad_up = grad_hidden * silu_gate
    grad_ff = jnp.concatenate([grad_gate.astype(bf16), grad_up.astype(bf16)], axis=1)
    grad_hat_two = scattered(mm_nt(grad_ff, ff_all))
    ff_grad = mm_tn(hat_two_seq, grad_ff).astype(bf16)
    grad_hat_two, ff_grad = lax.optimization_barrier((grad_hat_two, ff_grad))
    ff_grad, down_sum = lax.optimization_barrier((ff_grad, down_sum))
    ff_sum = summed(ff_grad)
    down_share = own_share(down_sum)
    grad_middle = grad_out + norm_back(grad_hat_two, hat_two, inv_two)

    grad_mid_seq = gathered(grad_middle.astype(bf16))
    late_hidden, grad_mid_seq = lax.optimization_barrier((hidden, grad_mid_seq))
    layer_out = unpermuted((middle + scattered(mm_nt(late_hidden, down_all))).astype(bf16))
    grad_heads = mm(grad_mid_seq, out_all).astype(bf16).reshape(seq_len, head_count, head_width)
    row_dot = jnp.sum(grad_heads.astype(f32) * attended, axis=2)
    grad_probs = jnp.einsum("thd,kd->htk", grad_heads, values, preferred_element_type=f32)
    grad_scores = (probs * (grad_probs - row_dot.T[:, :, None])).astype(bf16)
    grad_query = jnp.einsum("htk,kd->thd", grad_scores, keys, preferred_element_type=f32)
    grad_keys = jnp.einsum("htk,thd->kd", grad_scores, queries, preferred_element_type=f32)
    grad_values = jnp.einsum("htk,thd->kd", probs_low, grad_heads, preferred_element_type=f32)
    kv_total = scattered(jnp.concatenate([grad_keys, grad_values], axis=1))
    kv_total = kv_total + kv_grad[0].astype(f32)
    key_back = rotate_back(kv_total[:, :head_width], cos_own, sin_own)
    grad_kv_pre = jnp.concatenate([key_back, kv_total[:, head_width:]], axis=1).astype(bf16)
    query_back = rotate_back(grad_query * score_scale, cos_all[:, None, :], sin_all[:, None, :])
    grad_query_pre = query_back.reshape(seq_len, query_cols).astype(bf16)
    grad_hat_one = scattered(mm_nt(grad_query_pre, query_all)) + mm_nt(grad_kv_pre, kv_all)
    input_grad = unpermuted(grad_middle + norm_back(grad_hat_one, hat_one, inv_one))
    attn_grad = jnp.concatenate(
        [
            mm_tn(hat_one_seq, grad_query_pre).astype(bf16),
            mm_tn(hat_one_low, grad_kv_pre).astype(bf16),
            mm_tn(grad_mid_seq, attn_rows).astype(bf16),
        ],
        axis=1,
    )
    attn_grad, ff_sum = lax.optimization_barrier((attn_grad, ff_sum))
    ff_share = own_share(ff_sum)
    attn_share = own_share(summed(attn_grad))
    query_raw = joined(attn_share[:, :, :query_cols])
    kv_raw = jnp.sum(attn_share[:, :, query_cols : query_cols + kv_width], axis=0)
    out_weight_grad = joined(attn_share[:, :, query_cols + kv_width :])
    gate_raw = joined(ff_share[:, :, :ff_cols])
    up_raw = joined(ff_share[:, :, ff_cols:])

    def row_sum(raw, matrix):
        return jnp.sum(raw * matrix.astype(f32), axis=1)

    return (
        layer_out[None],
        shared[None],
        input_grad[None],
        row_sum(query_raw, query_weight) + row_sum(kv_raw, kv_weight),
        query_raw * gain_one,
        kv_raw * gain_one,
        out_weight_grad,
        row_sum(gate_raw, gate_weight) + row_sum(up_raw, up_weight),
        gate_raw * gain_two,
        up_raw * gain_two,
        joined(down_share),
    )


def solution(mesh):
    rows = P("fsdp", "dp", None)
    gain = P(("dp", "fsdp"))
    matrix = P(("dp", "fsdp"), None)
    return jax.shard_map(
        local,
        mesh=mesh,
        in_specs=(
            rows,
            gain,
            matrix,
            matrix,
            matrix,
            gain,
            matrix,
            matrix,
            matrix,
            P("fsdp"),
            P(),
            rows,
            rows,
        ),
        out_specs=(
            rows,
            rows,
            rows,
            gain,
            matrix,
            matrix,
            matrix,
            gain,
            matrix,
            matrix,
            matrix,
        ),
        check_vma=False,
    )
```

```python
import jax
import jax.numpy as jnp
from jax import lax
from jax.sharding import PartitionSpec as P

norm_eps = 1e-05
rope_base = 10000.0
masked_score = -1e30
f32 = jnp.float32
bf16 = jnp.bfloat16


def rope_tables(positions, half_width):
    index_vec = jnp.arange(half_width, dtype=f32)
    frequency = jnp.power(rope_base, -(2.0 * index_vec) / (2 * half_width))
    angles = positions.astype(f32)[:, None] * frequency[None, :]
    return (jnp.cos(angles), jnp.sin(angles))


def rotate(values, cos_vals, sin_vals):
    half_width = values.shape[-1] // 2
    first_half = values[..., :half_width]
    second_half = values[..., half_width:]
    return jnp.concatenate(
        [
            first_half * cos_vals - second_half * sin_vals,
            second_half * cos_vals + first_half * sin_vals,
        ],
        axis=-1,
    )


def rotate_back(values, cos_vals, sin_vals):
    return rotate(values, cos_vals, -sin_vals)


def norm_back(grad_hat, normed_hat, inv_rms):
    inner_mean = jnp.mean(grad_hat * normed_hat, axis=1, keepdims=True)
    return inv_rms * (grad_hat - normed_hat * inner_mean)


def mm(left, right):
    return jnp.dot(left, right, preferred_element_type=f32)


def mm_nt(left, right):
    return lax.dot_general(left, right, (((1,), (1,)), ((), ())), preferred_element_type=f32)


def mm_tn(left, right):
    return lax.dot_general(left, right, (((0,), (0,)), ((), ())), preferred_element_type=f32)


def local(
    tokens,
    attn_gain,
    query_weight,
    kv_weight,
    out_weight,
    mlp_gain,
    gate_weight,
    up_weight,
    down_weight,
    seq_group,
    group_weight,
    out_grad,
    kv_grad,
):
    dp_size = lax.axis_size("dp")
    fsdp_size = lax.axis_size("fsdp")
    dp_index = lax.axis_index("dp")
    tok_rows, model_width = tokens.shape[1:]
    own_rows = query_weight.shape[0]
    head_width = kv_weight.shape[1] // 2
    kv_width = 2 * head_width
    query_cols = query_weight.shape[1] // dp_size
    head_count = query_cols // head_width
    ff_cols = gate_weight.shape[1] // dp_size
    score_scale = head_width ** (-0.5)

    def permuted(rows):
        blocks = rows.reshape(rows.shape[0], dp_size, fsdp_size, own_rows)
        return blocks.transpose(0, 2, 1, 3).reshape(rows.shape)

    def unpermuted(rows):
        blocks = rows.reshape(rows.shape[0], fsdp_size, dp_size, own_rows)
        return blocks.transpose(0, 2, 1, 3).reshape(rows.shape)

    def peers(step):
        return [(i, i ^ step) for i in range(dp_size)]

    def gathered(block):
        blocks = [block] + [lax.ppermute(block, "dp", peers(k)) for k in range(1, dp_size)]
        return jnp.concatenate(blocks, axis=0)

    def scattered(partial):
        rows = partial.shape[0] // dp_size
        total = partial[:rows]
        for k in range(1, dp_size):
            part = partial[k * rows : (k + 1) * rows].astype(bf16)
            total = total + lax.ppermute(part, "dp", peers(k)).astype(f32)
        return total

    def column_blocks(matrix):
        cols = matrix.shape[1] // dp_size
        return matrix.reshape(own_rows, dp_size, cols).transpose(1, 0, 2)

    def exchanged(packed):
        return lax.all_to_all(packed, "dp", 0, 0)

    def all_rows(packed):
        return lax.all_gather(
            packed.reshape(dp_size * own_rows, packed.shape[2]), "fsdp", axis=0, tiled=True
        )

    def summed(grads):
        return lax.psum_scatter(grads.astype(bf16), "fsdp", scatter_dimension=0, tiled=True)

    def own_share(share):
        return exchanged(share.reshape(dp_size, own_rows, share.shape[1])).astype(f32)

    def joined(blocks):
        return blocks.transpose(1, 0, 2).reshape(own_rows, dp_size * blocks.shape[2])

    gain_one = attn_gain.astype(f32)[:, None]
    gain_two = mlp_gain.astype(f32)[:, None]

    def scaled(matrix, gain):
        return (matrix.astype(f32) * gain).astype(bf16)

    attn_pack = jnp.concatenate(
        [
            column_blocks(scaled(query_weight, gain_one)),
            jnp.broadcast_to(scaled(kv_weight, gain_one)[None], (dp_size, own_rows, kv_width)),
            column_blocks(out_weight),
        ],
        axis=2,
    )
    ff_pack = jnp.concatenate(
        [
            column_blocks(scaled(gate_weight, gain_two)),
            column_blocks(scaled(up_weight, gain_two)),
        ],
        axis=2,
    )
    attn_all = all_rows(exchanged(attn_pack))
    ff_all = all_rows(exchanged(ff_pack))
    down_all = all_rows(exchanged(column_blocks(down_weight)))
    query_all = attn_all[:, :query_cols]
    kv_all = attn_all[:, query_cols : query_cols + kv_width]
    out_all = attn_all[:, query_cols + kv_width :]

    def block_positions(k):
        return (dp_index ^ k) * tok_rows + jnp.arange(tok_rows, dtype=jnp.int32)

    positions = jnp.concatenate([block_positions(k) for k in range(dp_size)])
    cos_all, sin_all = rope_tables(positions, head_width // 2)
    cos_own, sin_own = cos_all[:tok_rows], sin_all[:tok_rows]
    seq_len = positions.shape[0]

    inputs = permuted(tokens[0]).astype(f32)
    inv_one = lax.rsqrt(jnp.mean(inputs * inputs, axis=1, keepdims=True) + norm_eps)
    hat_one = inputs * inv_one
    hat_one_low = hat_one.astype(bf16)
    hat_one_seq = gathered(hat_one_low)
    kv_pre = mm(hat_one_low, kv_all)
    key_rot = rotate(kv_pre[:, :head_width], cos_own, sin_own)
    shared = jnp.concatenate([key_rot, kv_pre[:, head_width:]], axis=1).astype(bf16)
    shared_seq = gathered(shared)
    keys, values = shared_seq[:, :head_width], shared_seq[:, head_width:]
    query_pre = mm(hat_one_seq, query_all).reshape(seq_len, head_count, head_width)
    query_rot = rotate(query_pre, cos_all[:, None, :], sin_all[:, None, :])
    queries = (query_rot * score_scale).astype(bf16)
    scores = jnp.einsum("thd,kd->htk", queries, keys, preferred_element_type=f32)
    visible = positions[None, :] <= positions[:, None]
    scores = jnp.where(visible[None], scores, masked_score)
    probs = jax.nn.softmax(scores, axis=-1)
    probs_low = probs.astype(bf16)
    attended = jnp.einsum("htk,kd->thd", probs_low, values, preferred_element_type=f32)
    attn_rows = attended.reshape(seq_len, query_cols).astype(bf16)
    middle = inputs + scattered(mm_nt(attn_rows, out_all))

    inv_two = lax.rsqrt(jnp.mean(middle * middle, axis=1, keepdims=True) + norm_eps)
    hat_two = middle * inv_two
    hat_two_seq = gathered(hat_two.astype(bf16))
    pre = mm(hat_two_seq, ff_all)
    gate_pre, up_pre = pre[:, :ff_cols], pre[:, ff_cols:]
    sigmoid_gate = jax.nn.sigmoid(gate_pre)
    silu_gate = gate_pre * sigmoid_gate
    hidden = (silu_gate * up_pre).astype(bf16)

    group_ids = jnp.arange(group_weight.shape[0], dtype=jnp.int32)
    seq_weight = jnp.sum(jnp.where(group_ids == seq_group[0], group_weight, 0.0))
    grad_out = permuted(out_grad[0]).astype(f32) * seq_weight
    grad_out_seq = gathered(grad_out.astype(bf16))
    down_grad = mm_tn(grad_out_seq, hidden).astype(bf16)
    down_all, down_grad = lax.optimization_barrier((down_all, down_grad))
    down_sum = summed(down_grad)
    grad_hidden = mm(grad_out_seq, down_all)
    grad_gate = grad_hidden * up_pre * sigmoid_gate * (1.0 + gate_pre * (1.0 - sigmoid_gate))
    grad_up = grad_hidden * silu_gate
    grad_ff = jnp.concatenate([grad_gate.astype(bf16), grad_up.astype(bf16)], axis=1)
    grad_hat_two = scattered(mm_nt(grad_ff, ff_all))
    ff_grad = mm_tn(hat_two_seq, grad_ff).astype(bf16)
    grad_hat_two, ff_grad = lax.optimization_barrier((grad_hat_two, ff_grad))
    ff_grad, down_sum = lax.optimization_barrier((ff_grad, down_sum))
    ff_sum = summed(ff_grad)
    down_share = own_share(down_sum)
    grad_middle = grad_out + norm_back(grad_hat_two, hat_two, inv_two)

    grad_mid_seq = gathered(grad_middle.astype(bf16))
    late_hidden, grad_mid_seq = lax.optimization_barrier((hidden, grad_mid_seq))
    layer_out = unpermuted((middle + scattered(mm_nt(late_hidden, down_all))).astype(bf16))
    grad_heads = mm(grad_mid_seq, out_all).astype(bf16).reshape(seq_len, head_count, head_width)
    row_dot = jnp.sum(grad_heads.astype(f32) * attended, axis=2)
    grad_probs = jnp.einsum("thd,kd->htk", grad_heads, values, preferred_element_type=f32)
    grad_scores = (probs * (grad_probs - row_dot.T[:, :, None])).astype(bf16)
    grad_query = jnp.einsum("htk,kd->thd", grad_scores, keys, preferred_element_type=f32)
    grad_keys = jnp.einsum("htk,thd->kd", grad_scores, queries, preferred_element_type=f32)
    grad_values = jnp.einsum("htk,thd->kd", probs_low, grad_heads, preferred_element_type=f32)
    kv_total = scattered(jnp.concatenate([grad_keys, grad_values], axis=1))
    kv_total = kv_total + kv_grad[0].astype(f32)
    key_back = rotate_back(kv_total[:, :head_width], cos_own, sin_own)
    grad_kv_pre = jnp.concatenate([key_back, kv_total[:, head_width:]], axis=1).astype(bf16)
    query_back = rotate_back(grad_query * score_scale, cos_all[:, None, :], sin_all[:, None, :])
    grad_query_pre = query_back.reshape(seq_len, query_cols).astype(bf16)
    grad_hat_one = scattered(mm_nt(grad_query_pre, query_all)) + mm_nt(grad_kv_pre, kv_all)
    attn_grad = jnp.concatenate(
        [
            mm_tn(hat_one_seq, grad_query_pre).astype(bf16),
            mm_tn(hat_one_low, grad_kv_pre).astype(bf16),
            mm_tn(grad_mid_seq, attn_rows).astype(bf16),
        ],
        axis=1,
    )
    attn_grad, ff_sum, grad_hat_one, layer_out = lax.optimization_barrier(
        (attn_grad, ff_sum, grad_hat_one, layer_out)
    )
    input_grad = unpermuted(grad_middle + norm_back(grad_hat_one, hat_one, inv_one))
    ff_share = own_share(ff_sum)
    attn_share = own_share(summed(attn_grad))
    query_raw = joined(attn_share[:, :, :query_cols])
    kv_raw = jnp.sum(attn_share[:, :, query_cols : query_cols + kv_width], axis=0)
    out_weight_grad = joined(attn_share[:, :, query_cols + kv_width :])
    gate_raw = joined(ff_share[:, :, :ff_cols])
    up_raw = joined(ff_share[:, :, ff_cols:])

    def row_sum(raw, matrix):
        return jnp.sum(raw * matrix.astype(f32), axis=1)

    return (
        layer_out[None],
        shared[None],
        input_grad[None],
        row_sum(query_raw, query_weight) + row_sum(kv_raw, kv_weight),
        query_raw * gain_one,
        kv_raw * gain_one,
        out_weight_grad,
        row_sum(gate_raw, gate_weight) + row_sum(up_raw, up_weight),
        gate_raw * gain_two,
        up_raw * gain_two,
        joined(down_share),
    )


def solution(mesh):
    rows = P("fsdp", "dp", None)
    gain = P(("dp", "fsdp"))
    matrix = P(("dp", "fsdp"), None)
    return jax.shard_map(
        local,
        mesh=mesh,
        in_specs=(
            rows,
            gain,
            matrix,
            matrix,
            matrix,
            gain,
            matrix,
            matrix,
            matrix,
            P("fsdp"),
            P(),
            rows,
            rows,
        ),
        out_specs=(
            rows,
            rows,
            rows,
            gain,
            matrix,
            matrix,
            matrix,
            gain,
            matrix,
            matrix,
            matrix,
        ),
        check_vma=False,
    )
```

```python
import jax
import jax.numpy as jnp
from jax import lax
from jax.sharding import PartitionSpec as P

norm_eps = 1e-05
rope_base = 10000.0
masked_score = -1e30
f32 = jnp.float32
bf16 = jnp.bfloat16


def rope_tables(positions, half_width):
    index_vec = jnp.arange(half_width, dtype=f32)
    frequency = jnp.power(rope_base, -(2.0 * index_vec) / (2 * half_width))
    angles = positions.astype(f32)[:, None] * frequency[None, :]
    return (jnp.cos(angles), jnp.sin(angles))


def rotate(values, cos_vals, sin_vals):
    half_width = values.shape[-1] // 2
    first_half = values[..., :half_width]
    second_half = values[..., half_width:]
    return jnp.concatenate(
        [
            first_half * cos_vals - second_half * sin_vals,
            second_half * cos_vals + first_half * sin_vals,
        ],
        axis=-1,
    )


def rotate_back(values, cos_vals, sin_vals):
    return rotate(values, cos_vals, -sin_vals)


def norm_back(grad_hat, normed_hat, inv_rms):
    inner_mean = jnp.mean(grad_hat * normed_hat, axis=1, keepdims=True)
    return inv_rms * (grad_hat - normed_hat * inner_mean)


def mm(left, right):
    return jnp.dot(left, right, preferred_element_type=f32)


def mm_nt(left, right):
    return lax.dot_general(left, right, (((1,), (1,)), ((), ())), preferred_element_type=f32)


def mm_tn(left, right):
    return lax.dot_general(left, right, (((0,), (0,)), ((), ())), preferred_element_type=f32)


def local(
    tokens,
    attn_gain,
    query_weight,
    kv_weight,
    out_weight,
    mlp_gain,
    gate_weight,
    up_weight,
    down_weight,
    seq_group,
    group_weight,
    out_grad,
    kv_grad,
):
    dp_size = lax.axis_size("dp")
    fsdp_size = lax.axis_size("fsdp")
    dp_index = lax.axis_index("dp")
    tok_rows, model_width = tokens.shape[1:]
    own_rows = query_weight.shape[0]
    head_width = kv_weight.shape[1] // 2
    kv_width = 2 * head_width
    query_cols = query_weight.shape[1] // dp_size
    head_count = query_cols // head_width
    ff_cols = gate_weight.shape[1] // dp_size
    score_scale = head_width ** (-0.5)

    def permuted(rows):
        blocks = rows.reshape(rows.shape[0], dp_size, fsdp_size, own_rows)
        return blocks.transpose(0, 2, 1, 3).reshape(rows.shape)

    def unpermuted(rows):
        blocks = rows.reshape(rows.shape[0], fsdp_size, dp_size, own_rows)
        return blocks.transpose(0, 2, 1, 3).reshape(rows.shape)

    def peers(step):
        return [(i, i ^ step) for i in range(dp_size)]

    def gathered(block):
        blocks = [block] + [lax.ppermute(block, "dp", peers(k)) for k in range(1, dp_size)]
        return jnp.concatenate(blocks, axis=0)

    def scattered(partial):
        rows = partial.shape[0] // dp_size
        total = partial[:rows]
        for k in range(1, dp_size):
            part = partial[k * rows : (k + 1) * rows].astype(bf16)
            total = total + lax.ppermute(part, "dp", peers(k)).astype(f32)
        return total

    def column_blocks(matrix):
        cols = matrix.shape[1] // dp_size
        return matrix.reshape(own_rows, dp_size, cols).transpose(1, 0, 2)

    def exchanged(packed):
        return lax.all_to_all(packed, "dp", 0, 0)

    def all_rows(packed):
        return lax.all_gather(
            packed.reshape(dp_size * own_rows, packed.shape[2]), "fsdp", axis=0, tiled=True
        )

    def summed(grads):
        return lax.psum_scatter(grads.astype(bf16), "fsdp", scatter_dimension=0, tiled=True)

    def own_share(share):
        return exchanged(share.reshape(dp_size, own_rows, share.shape[1])).astype(f32)

    pair_cols = head_width // (2 * dp_size)

    def kv_split(matrix):
        rows = matrix.shape[0]
        keys = matrix[:, :head_width].reshape(rows, 2, dp_size, pair_cols)
        vals = matrix[:, head_width:].reshape(rows, dp_size, 2 * pair_cols)
        keys = keys.transpose(2, 0, 1, 3).reshape(dp_size, rows, 2 * pair_cols)
        return jnp.concatenate([keys, vals.transpose(1, 0, 2)], axis=2)

    def kv_join(blocks):
        rows = blocks.shape[1]
        keys = blocks[:, :, : 2 * pair_cols].reshape(dp_size, rows, 2, pair_cols)
        keys = keys.transpose(1, 2, 0, 3).reshape(rows, head_width)
        vals = blocks[:, :, 2 * pair_cols :].transpose(1, 0, 2).reshape(rows, head_width)
        return jnp.concatenate([keys, vals], axis=1)

    def flipped(parts):
        parts = list(parts)
        for bit in [1 << j for j in range(dp_size.bit_length() - 1)]:
            flip = (dp_index & bit) != 0
            parts = [jnp.where(flip, parts[k ^ bit], parts[k]) for k in range(dp_size)]
        return parts

    def moved_rows(block, k):
        rows = block.shape[0] // dp_size
        return jnp.concatenate(
            [block[(k ^ m) * rows : (k ^ m) * rows + rows] for m in range(dp_size)], axis=0
        )

    def joined(blocks):
        return blocks.transpose(1, 0, 2).reshape(own_rows, dp_size * blocks.shape[2])

    gain_one = attn_gain.astype(f32)[:, None]
    gain_two = mlp_gain.astype(f32)[:, None]

    def scaled(matrix, gain):
        return (matrix.astype(f32) * gain).astype(bf16)

    attn_pack = jnp.concatenate(
        [
            column_blocks(scaled(query_weight, gain_one)),
            column_blocks(out_weight),
            kv_split(scaled(kv_weight, gain_one)),
        ],
        axis=2,
    )
    ff_pack = jnp.concatenate(
        [
            column_blocks(scaled(gate_weight, gain_two)),
            column_blocks(scaled(up_weight, gain_two)),
        ],
        axis=2,
    )
    attn_all = all_rows(exchanged(attn_pack))
    ff_all = all_rows(exchanged(ff_pack))
    down_all = all_rows(exchanged(column_blocks(down_weight)))
    query_all = attn_all[:, :query_cols]
    out_all = attn_all[:, query_cols : 2 * query_cols]
    kv_all = attn_all[:, 2 * query_cols :]

    def block_positions(k):
        return (dp_index ^ k) * tok_rows + jnp.arange(tok_rows, dtype=jnp.int32)

    positions = jnp.concatenate([block_positions(k) for k in range(dp_size)])
    cos_all, sin_all = rope_tables(positions, head_width // 2)
    cos_own = lax.dynamic_slice_in_dim(cos_all, dp_index * pair_cols, pair_cols, axis=1)
    sin_own = lax.dynamic_slice_in_dim(sin_all, dp_index * pair_cols, pair_cols, axis=1)
    seq_len = positions.shape[0]

    inputs = permuted(tokens[0]).astype(f32)
    inv_one = lax.rsqrt(jnp.mean(inputs * inputs, axis=1, keepdims=True) + norm_eps)
    hat_one = inputs * inv_one
    hat_one_low = hat_one.astype(bf16)
    hat_one_seq = gathered(hat_one_low)
    kv_pre = mm(hat_one_seq, kv_all)
    key_rot = rotate(kv_pre[:, : 2 * pair_cols], cos_own, sin_own)
    shared_cols = jnp.concatenate([key_rot, kv_pre[:, 2 * pair_cols :]], axis=1).astype(bf16)
    shared_parts = [shared_cols]
    for k in range(1, dp_size):
        shared_parts.append(moved_rows(lax.ppermute(shared_cols, "dp", peers(k)), k))
    shared_seq = kv_join(jnp.stack(flipped(shared_parts)))
    shared = shared_seq[:tok_rows]
    keys, values = shared_seq[:, :head_width], shared_seq[:, head_width:]
    query_pre = mm(hat_one_seq, query_all).reshape(seq_len, head_count, head_width)
    query_rot = rotate(query_pre, cos_all[:, None, :], sin_all[:, None, :])
    queries = (query_rot * score_scale).astype(bf16)
    scores = jnp.einsum("thd,kd->htk", queries, keys, preferred_element_type=f32)
    visible = positions[None, :] <= positions[:, None]
    scores = jnp.where(visible[None], scores, masked_score)
    probs = jax.nn.softmax(scores, axis=-1)
    probs_low = probs.astype(bf16)
    attended = jnp.einsum("htk,kd->thd", probs_low, values, preferred_element_type=f32)
    attn_rows = attended.reshape(seq_len, query_cols).astype(bf16)
    middle = inputs + scattered(mm_nt(attn_rows, out_all))

    inv_two = lax.rsqrt(jnp.mean(middle * middle, axis=1, keepdims=True) + norm_eps)
    hat_two = middle * inv_two
    hat_two_seq = gathered(hat_two.astype(bf16))
    pre = mm(hat_two_seq, ff_all)
    gate_pre, up_pre = pre[:, :ff_cols], pre[:, ff_cols:]
    sigmoid_gate = jax.nn.sigmoid(gate_pre)
    silu_gate = gate_pre * sigmoid_gate
    hidden = (silu_gate * up_pre).astype(bf16)

    group_ids = jnp.arange(group_weight.shape[0], dtype=jnp.int32)
    seq_weight = jnp.sum(jnp.where(group_ids == seq_group[0], group_weight, 0.0))
    grad_out = permuted(out_grad[0]).astype(f32) * seq_weight
    grad_out_seq = gathered(grad_out.astype(bf16))
    late_parts = flipped(kv_split(kv_grad[0]))
    late_parts = late_parts[:1] + [
        lax.ppermute(late_parts[k], "dp", peers(k)) for k in range(1, dp_size)
    ]
    kv_late = jnp.concatenate(late_parts, axis=0).astype(f32)
    down_grad = mm_tn(grad_out_seq, hidden).astype(bf16)
    down_all, down_grad = lax.optimization_barrier((down_all, down_grad))
    down_sum = summed(down_grad)
    grad_hidden = mm(grad_out_seq, down_all)
    grad_gate = grad_hidden * up_pre * sigmoid_gate * (1.0 + gate_pre * (1.0 - sigmoid_gate))
    grad_up = grad_hidden * silu_gate
    grad_ff = jnp.concatenate([grad_gate.astype(bf16), grad_up.astype(bf16)], axis=1)
    grad_hat_two = scattered(mm_nt(grad_ff, ff_all))
    ff_grad = mm_tn(hat_two_seq, grad_ff).astype(bf16)
    grad_hat_two, ff_grad = lax.optimization_barrier((grad_hat_two, ff_grad))
    ff_grad, down_sum = lax.optimization_barrier((ff_grad, down_sum))
    ff_sum = summed(ff_grad)
    down_share = own_share(down_sum)
    grad_middle = grad_out + norm_back(grad_hat_two, hat_two, inv_two)

    grad_mid_seq = gathered(grad_middle.astype(bf16))
    late_hidden, grad_mid_seq = lax.optimization_barrier((hidden, grad_mid_seq))
    layer_out = unpermuted((middle + scattered(mm_nt(late_hidden, down_all))).astype(bf16))
    grad_heads = mm(grad_mid_seq, out_all).astype(bf16).reshape(seq_len, head_count, head_width)
    row_dot = jnp.sum(grad_heads.astype(f32) * attended, axis=2)
    grad_probs = jnp.einsum("thd,kd->htk", grad_heads, values, preferred_element_type=f32)
    grad_scores = (probs * (grad_probs - row_dot.T[:, :, None])).astype(bf16)
    grad_query = jnp.einsum("htk,kd->thd", grad_scores, keys, preferred_element_type=f32)
    grad_keys = jnp.einsum("htk,thd->kd", grad_scores, queries, preferred_element_type=f32)
    grad_values = jnp.einsum("htk,thd->kd", probs_low, grad_heads, preferred_element_type=f32)
    kv_parts = flipped(kv_split(jnp.concatenate([grad_keys, grad_values], axis=1)))
    kv_total = kv_parts[0] + kv_late
    for k in range(1, dp_size):
        part = moved_rows(kv_parts[k].astype(bf16), k)
        kv_total = kv_total + lax.ppermute(part, "dp", peers(k)).astype(f32)
    key_back = rotate_back(kv_total[:, : 2 * pair_cols], cos_own, sin_own)
    grad_kv_pre = jnp.concatenate([key_back, kv_total[:, 2 * pair_cols :]], axis=1).astype(bf16)
    query_back = rotate_back(grad_query * score_scale, cos_all[:, None, :], sin_all[:, None, :])
    grad_query_pre = query_back.reshape(seq_len, query_cols).astype(bf16)
    grad_hat_one = mm_nt(grad_query_pre, query_all) + mm_nt(grad_kv_pre, kv_all)
    attn_grad = jnp.concatenate(
        [
            mm_tn(hat_one_seq, grad_query_pre).astype(bf16),
            mm_tn(grad_mid_seq, attn_rows).astype(bf16),
            mm_tn(hat_one_seq, grad_kv_pre).astype(bf16),
        ],
        axis=1,
    )
    attn_grad, ff_sum, grad_hat_one, layer_out = lax.optimization_barrier(
        (attn_grad, ff_sum, grad_hat_one, layer_out)
    )
    input_grad = unpermuted(grad_middle + norm_back(scattered(grad_hat_one), hat_one, inv_one))
    ff_share = own_share(ff_sum)
    attn_share = own_share(summed(attn_grad))
    query_raw = joined(attn_share[:, :, :query_cols])
    out_weight_grad = joined(attn_share[:, :, query_cols : 2 * query_cols])
    kv_raw = kv_join(attn_share[:, :, 2 * query_cols :])
    gate_raw = joined(ff_share[:, :, :ff_cols])
    up_raw = joined(ff_share[:, :, ff_cols:])

    def row_sum(raw, matrix):
        return jnp.sum(raw * matrix.astype(f32), axis=1)

    return (
        layer_out[None],
        shared[None],
        input_grad[None],
        row_sum(query_raw, query_weight) + row_sum(kv_raw, kv_weight),
        query_raw * gain_one,
        kv_raw * gain_one,
        out_weight_grad,
        row_sum(gate_raw, gate_weight) + row_sum(up_raw, up_weight),
        gate_raw * gain_two,
        up_raw * gain_two,
        joined(down_share),
    )


def solution(mesh):
    rows = P("fsdp", "dp", None)
    gain = P(("dp", "fsdp"))
    matrix = P(("dp", "fsdp"), None)
    return jax.shard_map(
        local,
        mesh=mesh,
        in_specs=(
            rows,
            gain,
            matrix,
            matrix,
            matrix,
            gain,
            matrix,
            matrix,
            matrix,
            P("fsdp"),
            P(),
            rows,
            rows,
        ),
        out_specs=(
            rows,
            rows,
            rows,
            gain,
            matrix,
            matrix,
            matrix,
            gain,
            matrix,
            matrix,
            matrix,
        ),
        check_vma=False,
    )
```
